32 devices in a mesh: dp: 4 (over x, core), expert: 8 (over z, y).
Axes of the slice: x: 2, y: 2, z: 4, core: 2. Of those that a mesh axis runs over, the one named last changes fastest.
Arguments:
- tokens: bfloat16 [2048, 2048], P(('dp', 'expert')), may hold values from -6 to 6
- gate_values: float32 [2048, 4], P(('dp', 'expert')), may hold values from 0.1 to 1
- chosen: int32 [2048, 4], P(('dp', 'expert')), may hold values from 0 to 63, all different within a row; in each aligned block of 64 rows (0 to 63, 64 to 127, ...) at most 8 rows name the same one
- slot_table: int32 [64], replicated, may hold values from 0 to 63, each once
- w_gate: bfloat16 [64, 768, 2048], P('expert', 'dp'), may hold values from -0.125 to 0.125
- w_up: bfloat16 [64, 768, 2048], P('expert', 'dp'), may hold values from -0.125 to 0.125
- w_down: bfloat16 [64, 768, 2048], P('expert', 'dp'), may hold values from -0.21875 to 0.21875
- cotangent: bfloat16 [2048, 2048], P(('dp', 'expert')), may hold values from -0.59765625 to 0.59765625
Outputs:
- mixed: bfloat16 [2048, 2048], P(('dp', 'expert'))
- token_grads: bfloat16 [2048, 2048], P(('dp', 'expert'))
- gate_grads: float32 [2048, 4], P(('dp', 'expert'))
- gate_weight_grad: bfloat16 [64, 768, 2048], P('expert', 'dp')
- up_weight_grad: bfloat16 [64, 768, 2048], P('expert', 'dp')
- down_weight_grad: bfloat16 [64, 768, 2048], P('expert', 'dp')
The draws below stay inside these ranges and needn't reach their ends.
Inputs may be any that keep to these rules, and one draw needn't show every extreme that they name: `chosen`: each row names 4 distinct experts. Within the rows of one device (aligned blocks of 64 tokens) no expert is named by more than 8 rows, and in every draw some expert is named by exactly 8 rows of some block. `slot_table`: A permutation of the storage indices.
All inputs are finite; a program needn't handle non-finite values.
Results may differ from the reference program's by a relative error of at most 0.009.
Values may be sent and summed in bfloat16 or wider, within the bound.
A program may use at most 384 MiB of HBM per device.

```python
import math
import jax
import jax.numpy as jnp
import numpy as np
from jax import lax

D = 2048
FF = 768
EXPERTS = 64
TOPK = 4
TOK_DEV = 64
CAP = 8
TOKENS = 2048
N_DP = 4
N_EXPERT = 8


def block_levels(key, dims, pieces, smallest, largest):
    def one(axis_at, blocks):
        steps = jax.random.uniform(jax.random.fold_in(jax.random.fold_in(key, 6), axis_at), (blocks,), jnp.float32, smallest / len(pieces), largest / len(pieces))
        return jnp.repeat(jnp.exp(steps), dims[axis_at] // blocks).reshape((-1,) + (1,) * (len(dims) - axis_at - 1))

    factor_of = one(*pieces[0])
    for cut in pieces[1:]:
        factor_of = factor_of * one(*cut)
    return factor_of


def deal_out(stream_key, own, number, rows, amount, top, limit, lean):
    sequence = jax.random.permutation(stream_key, amount)
    crowded, ordinary = shares(amount, rows * top, limit, lean, True), shares(amount, rows * top, limit, lean, False)
    places = jnp.arange(amount)

    def named(tallies, offset_by):
        used = int((tallies > 0).sum())
        fixed = max(1, used // 4)
        passed = fixed + (places - fixed + offset_by * (used - fixed)) % max(1, amount - fixed)
        return jnp.zeros((amount,), jnp.int32).at[sequence[jnp.where(places < fixed, places, passed)]].set(jnp.asarray(tallies, jnp.int32))

    tallies = jnp.where(number % 4 == 0, named(crowded, number // 4), named(ordinary, number - number // 4 - 1))
    mixed = jax.random.permutation(jax.random.fold_in(own, 3), amount)
    donor, sink = mixed[0:amount // 2 * 2:2], mixed[1:amount // 2 * 2:2]
    slack = jnp.minimum(tallies[donor] - 1, limit - tallies[sink]) // 2
    slack = jnp.where((donor == sequence[0]) | (sink == sequence[0]) | (tallies[sink] == 0), 0, jnp.maximum(slack, 0))
    passed = jax.random.randint(jax.random.fold_in(own, 4), (amount // 2,), 0, 1 << 20) % (slack + 1)
    tallies = tallies.at[donor].add(-passed).at[sink].add(passed)
    labels = jnp.searchsorted(jnp.cumsum(tallies), jnp.arange(rows * top), side="right").astype(jnp.int32)
    table = labels.reshape(top, rows).T
    table = table[jax.random.permutation(jax.random.fold_in(own, 1), rows)]
    offset_by = jax.random.randint(jax.random.fold_in(own, 2), (rows, 1), 0, top)
    return jnp.take_along_axis(table, (jnp.arange(top)[None, :] + offset_by) % top, axis=1)


def shares(count, total, bound, skew, full):
    loads = [(1 << 20) // math.isqrt(standing ** skew) + 1 for standing in range(1, count + 1)]
    largest = bound if full else min(bound, max(-(-total // count), total * loads[0] // sum(loads)))
    least = 1 if total - largest >= count - 1 else 0
    holding, spare = [largest] + [least] * (count - 1), total - largest - least * (count - 1)
    while spare > 0:
        free = [i for i in range(1, count) if holding[i] < largest] or [i for i in range(1, count) if holding[i] < bound]
        mass, budget = sum([loads[i] for i in free]), spare
        for i in free:
            more = min(bound - holding[i], max(1, budget * loads[i] // mass), spare)
            holding[i] = holding[i] + more
            spare = spare - more
    return np.array(holding)


def normal_values(rng, extent, deviation, most, cuts=(), kind=jnp.bfloat16):
    result = jax.random.normal(rng, extent, jnp.float32) * deviation
    if len(cuts) > 0:
        result = block_levels(rng, extent, cuts, -0.22, 0.18) * result
    return jnp.clip(result, min=-most, max=most).astype(kind)


def setup_inputs(seed: int = 0) -> dict:
    seeds = jax.random.split(jax.random.key(seed), 9)
    tokens = normal_values(seeds[0], (TOKENS, D), 1.0, 6.0, ((0, 32),))
    gate_values = jnp.clip(0.1 + 0.9 * jax.random.uniform(seeds[1], (TOKENS, TOPK), jnp.float32) ** block_levels(seeds[1], (TOKENS, TOPK), ((0, 32),), -0.2, 0.2), 0.1, 1.0)
    chosen_keys = jax.random.split(jax.random.fold_in(seeds[2], 1), TOKENS // TOK_DEV)
    chosen_turns = jax.random.permutation(jax.random.fold_in(seeds[2], 3), TOKENS // TOK_DEV)
    chosen = jax.vmap(lambda own, number: deal_out(jax.random.fold_in(seeds[2], 2), own, number, TOK_DEV, EXPERTS, TOPK, CAP, 2))(chosen_keys, chosen_turns).reshape((TOKENS, TOPK))
    slot_table = jax.random.permutation(seeds[3], EXPERTS).astype(jnp.int32)
    w_gate = normal_values(seeds[4], (EXPERTS, FF, D), D ** -0.5, 0.125, ((0, 8), (1, 4)))
    w_up = normal_values(seeds[5], (EXPERTS, FF, D), D ** -0.5, 0.125, ((0, 8), (1, 4)))
    w_down = normal_values(seeds[6], (EXPERTS, FF, D), FF ** -0.5, 0.21875, ((0, 8), (1, 4)))
    cotangent = normal_values(seeds[7], (TOKENS, D), 0.1, 0.59765625, ((0, 32),))
    return {"tokens": tokens, "gate_values": gate_values, "chosen": chosen, "slot_table": slot_table, "w_gate": w_gate, "w_up": w_up, "w_down": w_down, "cotangent": cotangent}


def group_grad(left_rows, right_rows):
    left_rows = left_rows.reshape(N_DP, -1, left_rows.shape[-1]).astype(jnp.float32)
    right_rows = right_rows.reshape(N_DP, -1, right_rows.shape[-1]).astype(jnp.float32)
    partial_value = jnp.einsum('gmf,gmd->gfd', left_rows, right_rows).astype(jnp.bfloat16)
    partial_value = lax.optimization_barrier(partial_value)
    return lax.optimization_barrier(jnp.sum(partial_value.astype(jnp.float32), axis=0)).astype(jnp.bfloat16)

def reference(tokens, gate_values, chosen, slot_table, w_gate, w_up, w_down, cotangent):
    token_total = tokens.shape[0]
    assigned = token_total * TOPK
    slot_ids = slot_table[chosen].reshape(-1).astype(jnp.int32)
    device_rows = TOK_DEV * TOPK
    by_device = slot_ids.reshape(-1, device_rows)
    onehot = (by_device[:, :, None] == jnp.arange(EXPERTS, dtype=jnp.int32)).astype(jnp.int32)
    earlier = jnp.cumsum(onehot, axis=1) - onehot
    position = lax.optimization_barrier(jnp.sum(earlier * onehot, axis=2)).reshape(-1).astype(jnp.int32)
    assign_ids = jnp.arange(assigned, dtype=jnp.int32)
    owner_dev = assign_ids // device_rows
    source = owner_dev % N_EXPERT
    group_ids = owner_dev // N_EXPERT
    buffer_pos = ((slot_ids * N_DP + group_ids) * N_EXPERT + source) * CAP + position
    slot_rows = jnp.full((EXPERTS * N_DP * N_EXPERT * CAP,), assigned, jnp.int32)
    slot_rows = slot_rows.at[buffer_pos].set(assign_ids)
    slot_rows = slot_rows.reshape(EXPERTS, N_DP, N_EXPERT * CAP)
    tok_pad = jnp.concatenate([tokens, jnp.zeros((1, D), jnp.bfloat16)], axis=0)
    cot_pad = jnp.concatenate([cotangent, jnp.zeros((1, D), jnp.bfloat16)], axis=0)
    gate_pad = jnp.concatenate([gate_values.reshape(-1), jnp.zeros((1,), jnp.float32)], axis=0)

    def per_slot(packed):
        these_rows, gate_mat, up_mat, down_mat = packed
        token_ids = (these_rows // TOPK).astype(jnp.int32)
        rows_in = tok_pad[token_ids].reshape(-1, D)
        out_grads = (gate_pad[these_rows][..., None] * cot_pad[token_ids].astype(jnp.float32)).astype(jnp.bfloat16).reshape(-1, D)
        pre_gate = jnp.dot(rows_in, gate_mat.T, preferred_element_type=jnp.float32)
        pre_up = jnp.dot(rows_in, up_mat.T, preferred_element_type=jnp.float32)
        sigmoid_gate = jax.nn.sigmoid(pre_gate)
        hidden = (pre_gate * sigmoid_gate * pre_up).astype(jnp.bfloat16)
        expert_out = jnp.dot(hidden, down_mat, preferred_element_type=jnp.float32).astype(jnp.bfloat16)
        dhidden = jnp.dot(out_grads, down_mat.T, preferred_element_type=jnp.float32)
        grad_gate = (dhidden * pre_up * sigmoid_gate * (1.0 + pre_gate * (1.0 - sigmoid_gate))).astype(jnp.bfloat16)
        grad_up = (dhidden * pre_gate * sigmoid_gate).astype(jnp.bfloat16)
        back_rows = (jnp.dot(grad_gate, gate_mat, preferred_element_type=jnp.float32) + jnp.dot(grad_up, up_mat, preferred_element_type=jnp.float32)).astype(jnp.bfloat16)
        return (expert_out, back_rows, group_grad(grad_gate, rows_in), group_grad(grad_up, rows_in), group_grad(hidden, out_grads))
    expert_out, back_rows, gate_weight_grad, up_weight_grad, down_weight_grad = lax.map(per_slot, (slot_rows, w_gate, w_up, w_down))
    flat_rows = slot_rows.reshape(-1)
    out_table = jnp.zeros((assigned + 1, D), jnp.bfloat16).at[flat_rows].set(expert_out.reshape(-1, D))
    back_table = jnp.zeros((assigned + 1, D), jnp.bfloat16).at[flat_rows].set(back_rows.reshape(-1, D))
    out_tok = out_table[:assigned].reshape(token_total, TOPK, D)
    back_tok = back_table[:assigned].reshape(token_total, TOPK, D)
    mixed = lax.optimization_barrier(jnp.sum(gate_values[..., None] * out_tok.astype(jnp.float32), axis=1)).astype(jnp.bfloat16)
    gate_grads = jnp.einsum('td,tkd->tk', cotangent.astype(jnp.float32), out_tok.astype(jnp.float32))
    token_grads = lax.optimization_barrier(jnp.sum(back_tok.astype(jnp.float32), axis=1)).astype(jnp.bfloat16)
    return (mixed, token_grads, gate_grads, gate_weight_grad, up_weight_grad, down_weight_grad)
```

```python
import jax
import jax.numpy as jnp
from jax import lax
from jax.sharding import PartitionSpec as P

CAP = 8
PAD = 128
F32 = jnp.float32
BF16 = jnp.bfloat16
AXES = ("dp", "expert")


def split3(v):
    a = lax.reduce_precision(v, 8, 7)
    r = v - a
    b = lax.reduce_precision(r, 8, 7)
    return a.astype(BF16), b.astype(BF16), (r - b).astype(BF16)


def per_device(tokens, gate_values, chosen, slot_table, w_gate, w_up, w_down, cotangent):
    tok, width = tokens.shape
    topk = chosen.shape[1]
    experts = slot_table.shape[0]
    groups = lax.axis_size("expert")
    n_dev = groups * lax.axis_size("dp")
    per_dev = w_gate.shape[0]
    blocks = max(1, min(n_dev, 256 // tok))
    chunks = n_dev // blocks
    labels = jnp.arange(experts, dtype=jnp.int32)
    slot = jnp.sum(jnp.where(chosen[:, :, None] == labels, slot_table, 0), axis=2)
    named = jnp.sum((slot[:, :, None] == labels).astype(F32), axis=1)
    lower = (jnp.arange(tok)[:, None] > jnp.arange(tok)[None, :]).astype(F32)
    before = jnp.dot(lower, named, preferred_element_type=F32)
    pos = jnp.sum(jnp.where(slot[:, :, None] == labels, before[:, None, :], 0.0), axis=2)
    g1, g2, g3 = split3(gate_values)
    extra = jnp.concatenate([slot.astype(BF16), pos.astype(BF16), g1, g2, g3], axis=1)
    extra = jnp.pad(extra, ((0, 0), (0, PAD - extra.shape[1])))
    packed = jnp.concatenate([tokens, cotangent, extra], axis=1)
    allp = lax.all_gather(packed, AXES, axis=0, tiled=True)
    allp = allp.reshape(chunks, blocks * tok, 2 * width + PAD)
    x_all = allp[:, :, :width]
    c_all = allp[:, :, width : 2 * width]
    ex = allp[:, :, 2 * width : 2 * width + 5 * topk].astype(F32)
    ex = ex.reshape(chunks, blocks * tok, 5, topk)
    slot_all = ex[:, :, 0].astype(jnp.int32) - lax.axis_index("expert") * per_dev
    pos_all = ex[:, :, 1].astype(jnp.int32)
    gate_all = ex[:, :, 2] + ex[:, :, 3] + ex[:, :, 4]
    blk = (jnp.arange(blocks * tok, dtype=jnp.int32) // tok)[None, :, None]
    rows = blocks * CAP
    here = (slot_all >= 0) & (slot_all < per_dev)
    row_id = jnp.where(here, slot_all * rows + blk * CAP + pos_all, -1)
    rid = jnp.arange(per_dev * rows, dtype=jnp.int32)[None, :, None, None]
    match = row_id[:, None, :, :] == rid
    sel = jnp.sum(match.astype(F32), axis=3).astype(BF16)
    gate_row = jnp.sum(jnp.where(match, gate_all[:, None], 0.0), axis=(2, 3))

    def to_expert(v):
        v = v.reshape((chunks, per_dev, rows) + v.shape[2:])
        v = jnp.swapaxes(v, 0, 1)
        return v.reshape((per_dev, chunks * rows) + v.shape[3:])

    def to_chunk(v):
        v = v.reshape((per_dev, chunks, rows) + v.shape[2:])
        v = jnp.swapaxes(v, 0, 1)
        return v.reshape((chunks, per_dev * rows) + v.shape[3:])

    x_rows = to_expert(jnp.einsum("crt,ctd->crd", sel, x_all, preferred_element_type=F32).astype(BF16))
    c_rows = to_expert(jnp.einsum("crt,ctd->crd", sel, c_all, preferred_element_type=F32).astype(BF16))
    gate_e = to_expert(gate_row)[:, :, None]
    pre_gate = jnp.einsum("erd,efd->erf", x_rows, w_gate, preferred_element_type=F32)
    pre_up = jnp.einsum("erd,efd->erf", x_rows, w_up, preferred_element_type=F32)
    dh = jnp.einsum("erd,efd->erf", c_rows, w_down, preferred_element_type=F32)
    s = jax.nn.sigmoid(pre_gate)
    act = pre_gate * s
    hid = act * pre_up
    gg_row = jnp.sum(hid * dh, axis=2)
    hid = (hid * gate_e).astype(BF16)
    dh = dh * gate_e
    grad_gate = (dh * pre_up * s * (1.0 + pre_gate * (1.0 - s))).astype(BF16)
    grad_up = (dh * act).astype(BF16)
    out_rows = jnp.einsum("erf,efd->erd", hid, w_down, preferred_element_type=F32).astype(BF16)
    back_rows = (
        jnp.einsum("erf,efd->erd", grad_gate, w_gate, preferred_element_type=F32)
        + jnp.einsum("erf,efd->erd", grad_up, w_up, preferred_element_type=F32)
    ).astype(BF16)
    dw_gate = jnp.einsum("erf,erd->efd", grad_gate, x_rows, preferred_element_type=F32).astype(BF16)
    dw_up = jnp.einsum("erf,erd->efd", grad_up, x_rows, preferred_element_type=F32).astype(BF16)
    dw_down = jnp.einsum("erf,erd->efd", hid, c_rows, preferred_element_type=F32).astype(BF16)
    part_m = jnp.einsum("crt,crd->ctd", sel, to_chunk(out_rows), preferred_element_type=F32)
    part_b = jnp.einsum("crt,crd->ctd", sel, to_chunk(back_rows), preferred_element_type=F32)
    gg_c = to_chunk(gg_row)
    part_g = jnp.sum(jnp.where(match, gg_c[:, :, None, None], 0.0), axis=1)
    part_g = jnp.pad(part_g, ((0, 0), (0, 0), (0, PAD - topk)))
    part = jnp.concatenate([part_m.astype(BF16), part_b.astype(BF16), part_g.astype(BF16)], axis=2)
    part = part.reshape(n_dev * tok, 2 * width + PAD)
    red = lax.psum_scatter(part, AXES, scatter_dimension=0, tiled=True)
    return (
        red[:, :width],
        red[:, width : 2 * width],
        red[:, 2 * width : 2 * width + topk].astype(F32),
        dw_gate,
        dw_up,
        dw_down,
    )


def solution(mesh):
    tok = P(AXES, None)
    w = P("expert", "dp", None)
    return jax.shard_map(
        per_device,
        mesh=mesh,
        in_specs=(tok, tok, tok, P(), w, w, w, tok),
        out_specs=(tok, tok, tok, w, w, w),
        check_vma=False,
    )
```

```python
import functools

import jax
import jax.numpy as jnp
from jax import lax
from jax.experimental import pallas as pl
from jax.experimental.pallas import tpu as pltpu
from jax.sharding import PartitionSpec as P

CAP = 8
PAD = 128
F32 = jnp.float32
BF16 = jnp.bfloat16
AXES = ("dp", "expert")
VMEM_LIMIT = 60 * 1024 * 1024


def split3(v):
    a = lax.reduce_precision(v, 8, 7)
    r = v - a
    b = lax.reduce_precision(r, 8, 7)
    return a.astype(BF16), b.astype(BF16), (r - b).astype(BF16)


def nt(a, b):
    return lax.dot_general(a, b, (((1,), (1,)), ((), ())), preferred_element_type=F32)


def tn(a, b):
    return lax.dot_general(a, b, (((0,), (0,)), ((), ())), preferred_element_type=F32)


def nn(a, b):
    return jnp.dot(a, b, preferred_element_type=F32)


def expert_kernel(
    chunks, per_dev, rows, topk, x_ref, c_ref, rid_ref, gv_ref, wg_ref, wu_ref, wd_ref,
    part_ref, dwg_ref, dwu_ref, dwd_ref, xs, cs, sel_s, gate_s, gg_s,
):
    i = pl.program_id(0)
    toks, width = x_ref.shape
    m = per_dev * rows
    rid = lax.broadcasted_iota(jnp.int32, (m, toks), 0)

    @pl.when(i < chunks)
    def _():
        off = pl.multiple_of(i * rows, rows)
        sel = jnp.zeros((m, toks), F32)
        gate = jnp.zeros((m, toks), F32)
        for k in range(topk):
            hit = rid_ref[0, k : k + 1, :] == rid
            sel = jnp.where(hit, 1.0, sel)
            gate = jnp.where(hit, gv_ref[0, k : k + 1, :], gate)
        sel = sel.astype(BF16)
        gate_col = jnp.sum(gate, axis=1, keepdims=True)
        sel_s[i] = sel
        xr = nn(sel, x_ref[...]).astype(BF16)
        cr = nn(sel, c_ref[...]).astype(BF16)
        for e in range(per_dev):
            cut = slice(e * rows, (e + 1) * rows)
            xs[e, pl.ds(off, rows), :] = xr[cut]
            cs[e, pl.ds(off, rows), :] = cr[cut]
            gate_s[e, pl.ds(off, rows), :] = gate_col[cut]

    @pl.when((i >= chunks) & (i < chunks + per_dev))
    def _():
        e = i - chunks
        wg = wg_ref[0]
        wu = wu_ref[0]
        wd = wd_ref[0]
        full = xs.shape[1]
        step = min(256, full)
        tiles = full // step

        def tile(r, acc):
            cut = pl.ds(r if isinstance(r, int) else pl.multiple_of(r, step), step)
            xr = xs[e, cut, :]
            cr = cs[e, cut, :]
            gate = gate_s[e, cut, :]
            pre_gate = nt(xr, wg)
            pre_up = nt(xr, wu)
            dh = nt(cr, wd)
            s = jax.nn.sigmoid(pre_gate)
            act = pre_gate * s
            hid = act * pre_up
            gg_s[e, cut, :] = jnp.sum(hid * dh, axis=1, keepdims=True)
            hid = (hid * gate).astype(BF16)
            dh = dh * gate
            grad_gate = (dh * pre_up * s * (1.0 + pre_gate * (1.0 - s))).astype(BF16)
            grad_up = (dh * act).astype(BF16)
            new = (tn(grad_gate, xr), tn(grad_up, xr), tn(hid, cr))
            if acc is not None:
                new = tuple(p + q for p, q in zip(acc, new))
            xs[e, cut, :] = nn(hid, wd).astype(BF16)
            cs[e, cut, :] = (nn(grad_gate, wg) + nn(grad_up, wu)).astype(BF16)
            return new

        acc = tile(0, None)
        if tiles > 1:
            acc = lax.fori_loop(1, tiles, lambda j, c: tile(j * step, c), acc)
        dwg_ref[0] = acc[0].astype(BF16)
        dwu_ref[0] = acc[1].astype(BF16)
        dwd_ref[0] = acc[2].astype(BF16)

    @pl.when(i >= chunks + per_dev)
    def _():
        c = i - (chunks + per_dev)
        off = pl.multiple_of(c * rows, rows)
        sel = sel_s[c]
        outs = xs[:, pl.ds(off, rows), :].reshape(m, width)
        backs = cs[:, pl.ds(off, rows), :].reshape(m, width)
        part_ref[:, :width] = tn(sel, outs).astype(BF16)
        part_ref[:, width : 2 * width] = tn(sel, backs).astype(BF16)
        gg = gg_s[:, pl.ds(off, rows), :].reshape(m, 1)
        picks = [
            jnp.sum(jnp.where(rid_ref[0, k : k + 1, :] == rid, gg, 0.0), axis=0, keepdims=True)
            for k in range(topk)
        ]
        picks.append(jnp.zeros((PAD - topk, toks), F32))
        part_ref[:, 2 * width :] = jnp.concatenate(picks, axis=0).T.astype(BF16)


def experts_on_tokens(allp, row_id, gate_all, w_gate, w_up, w_down, width, chunks, rows):
    per_dev, ff, _ = w_gate.shape
    toks = allp.shape[0] // chunks
    topk = row_id.shape[1]
    kp = -(-topk // 8) * 8
    row_id = jnp.pad(row_id, ((0, 0), (0, kp - topk), (0, 0)), constant_values=-1)
    gate_all = jnp.pad(gate_all, ((0, 0), (0, kp - topk), (0, 0)))
    m = per_dev * rows
    full = chunks * rows

    def first(i):
        return jnp.minimum(i, chunks - 1)

    def mid(i):
        return jnp.clip(i - chunks, 0, per_dev - 1)

    def last(i):
        return jnp.clip(i - chunks - per_dev, 0, chunks - 1)

    def either(i):
        return jnp.where(i < chunks + per_dev, first(i), last(i))

    w_spec = pl.BlockSpec((1, ff, width), lambda i: (mid(i), 0, 0))
    small = pl.BlockSpec((1, kp, toks), lambda i: (either(i), 0, 0))
    dw = jax.ShapeDtypeStruct(w_gate.shape, BF16)
    return pl.pallas_call(
        functools.partial(expert_kernel, chunks, per_dev, rows, topk),
        grid=(2 * chunks + per_dev,),
        in_specs=[
            pl.BlockSpec((toks, width), lambda i: (first(i), 0)),
            pl.BlockSpec((toks, width), lambda i: (first(i), 1)),
            small,
            small,
            w_spec,
            w_spec,
            w_spec,
        ],
        out_specs=[
            pl.BlockSpec((toks, 2 * width + PAD), lambda i: (last(i), 0)),
            w_spec,
            w_spec,
            w_spec,
        ],
        out_shape=[jax.ShapeDtypeStruct((chunks * toks, 2 * width + PAD), BF16), dw, dw, dw],
        scratch_shapes=[
            pltpu.VMEM((per_dev, full, width), BF16),
            pltpu.VMEM((per_dev, full, width), BF16),
            pltpu.VMEM((chunks, m, toks), BF16),
            pltpu.VMEM((per_dev, full, 1), F32),
            pltpu.VMEM((per_dev, full, 1), F32),
        ],
        compiler_params=pltpu.CompilerParams(vmem_limit_bytes=VMEM_LIMIT),
    )(allp, allp, row_id, gate_all, w_gate, w_up, w_down)


def gather_all(packed):
    return lax.all_gather(packed, AXES, axis=0, tiled=True)


def scatter_all(part):
    return lax.psum_scatter(part, AXES, scatter_dimension=0, tiled=True)


def per_device(tokens, gate_values, chosen, slot_table, w_gate, w_up, w_down, cotangent):
    tok, width = tokens.shape
    topk = chosen.shape[1]
    experts = slot_table.shape[0]
    groups = lax.axis_size("expert")
    n_dev = groups * lax.axis_size("dp")
    per_dev = w_gate.shape[0]
    blocks = max(1, min(n_dev, 256 // tok))
    chunks = n_dev // blocks
    labels = jnp.arange(experts, dtype=jnp.int32)
    slot = jnp.sum(jnp.where(chosen[:, :, None] == labels, slot_table, 0), axis=2)
    named = jnp.sum((slot[:, :, None] == labels).astype(F32), axis=1)
    lower = (jnp.arange(tok)[:, None] > jnp.arange(tok)[None, :]).astype(F32)
    before = jnp.dot(lower, named, preferred_element_type=F32)
    pos = jnp.sum(jnp.where(slot[:, :, None] == labels, before[:, None, :], 0.0), axis=2)
    g1, g2, g3 = split3(gate_values)
    extra = jnp.concatenate([slot.astype(BF16), pos.astype(BF16), g1, g2, g3], axis=1)
    extra = jnp.pad(extra, ((0, 0), (0, PAD - extra.shape[1])))
    packed = jnp.concatenate([tokens, cotangent, extra], axis=1)
    allp = gather_all(packed)
    rows = blocks * CAP
    ex = allp[:, 2 * width :].astype(F32).reshape(chunks, blocks * tok, PAD)
    ex = jnp.swapaxes(ex, 1, 2)[:, : 5 * topk].reshape(chunks, 5, topk, blocks * tok)
    slot_all = ex[:, 0].astype(jnp.int32) - lax.axis_index("expert") * per_dev
    pos_all = ex[:, 1].astype(jnp.int32)
    gate_all = ex[:, 2] + ex[:, 3] + ex[:, 4]
    blk = jnp.arange(blocks * tok, dtype=jnp.int32) // tok
    here = (slot_all >= 0) & (slot_all < per_dev)
    row_id = jnp.where(here, slot_all * rows + blk * CAP + pos_all, -1)
    part, dw_gate, dw_up, dw_down = experts_on_tokens(
        allp, row_id, gate_all, w_gate, w_up, w_down, width, chunks, rows
    )
    red = scatter_all(part)
    return (
        red[:, :width],
        red[:, width : 2 * width],
        red[:, 2 * width : 2 * width + topk].astype(F32),
        dw_gate,
        dw_up,
        dw_down,
    )


def solution(mesh):
    tok = P(AXES, None)
    w = P("expert", "dp", None)
    return jax.shard_map(
        per_device,
        mesh=mesh,
        in_specs=(tok, tok, tok, P(), w, w, w, tok),
        out_specs=(tok, tok, tok, w, w, w),
        check_vma=False,
    )
```
